256 devices in a mesh: seq: 32 (over z, x), chan: 8 (over y, core).
Axes of the slice: x: 4, y: 4, z: 8, core: 2. Of those that a mesh axis runs over, the one named last changes fastest.
Arguments:
- token_ids: int32 [8192], P('seq'), may hold values from 0 to 511
- embed_table: bfloat16 [512, 8192], P(None, 'chan'), may hold values from -6 to 6
- se_query: bfloat16 [8192, 8192], P('seq', 'chan'), may hold values from -3 to 3
- se_key: bfloat16 [8192, 8192], P('seq', 'chan'), may hold values from -6 to 6
- se_filter: bfloat16 [512, 7], P('chan'), may hold values from -2 to 2
- mr_query: bfloat16 [8192, 8192], P('seq', 'chan'), may hold values from -3 to 3
- mr_key: bfloat16 [8192, 8192], P('seq', 'chan'), may hold values from -6 to 6
- mr_filter: bfloat16 [512, 128], P('chan'), may hold values from -0.5 to 0.5
- li_query: bfloat16 [8192, 8192], P('seq', 'chan'), may hold values from -3 to 3
- li_key: bfloat16 [8192, 8192], P('seq', 'chan'), may hold values from -6 to 6
- li_rate: float32 [512, 16], P('chan'), may hold values from 1.2207031e-06 to 0.05
- li_residue: float32 [512, 16], P('chan'), may hold values from -1.5 to 1.5
- attn_query: bfloat16 [8192, 8192], P('seq', 'chan'), may hold values from -7 to 7
- attn_key: bfloat16 [8192, 8192], P('seq', 'chan'), may hold values from -7 to 7
Outputs:
- block_out: bfloat16 [8192, 8192], P('seq', 'chan')
The draws below stay inside these ranges and needn't reach their ends.
All inputs are finite; a program needn't handle non-finite values.
Results may differ from the reference program's by a relative error of at most 0.01.
Values may be sent and summed in bfloat16 or wider, within the bound.
No kernel may reach another device: no remote copies, remote signals or barrier semaphores. Data moves between devices by JAX's collectives and lax.ppermute only.
A program may use at most 192 MiB of HBM per device.

```python
import math
import jax
import jax.numpy as jnp
import numpy as np
from jax import lax

D = 8192
HEAD_DIM = 128
VOCAB = 512
GROUP_CH = 16
SE_LEN = 7
MR_LEN = 128
STATE = 16
TOTAL = 8192
HEADS = 64
GROUPS = 512


def attention_pair(key):
    query_seed = jax.random.fold_in(key, 101)
    key_seed = jax.random.fold_in(key, 202)
    queries = jnp.clip(1.5 * jax.random.normal(query_seed, (TOTAL, D), jnp.float32), -7.0, 7.0)
    keys_drawn = jnp.clip(1.5 * jax.random.normal(key_seed, (TOTAL, D), jnp.float32), -7.0, 7.0)
    return (queries, keys_drawn)


def draw_attn_query(key, part):
    return attention_pair(key)[0].astype(jnp.bfloat16)


def draw_attn_key(key, part):
    return attention_pair(key)[1].astype(jnp.bfloat16)


def with_ends(values, key, smallest, top_value):
    longest = values.shape.index(max(values.shape))
    spots = []
    for shift in (0, 1):
        where = [jax.random.randint(jax.random.fold_in(key, axis), (), 0, length) for axis, length in enumerate(values.shape)]
        where[longest] = (where[longest] + shift) % values.shape[longest]
        spots.append(tuple(where))
    return values.at[spots[0]].set(smallest).at[spots[1]].set(top_value)


def shard_levels(rng, extent, cuts, low, largest):
    level, own = 1.0, jax.random.fold_in(rng, 6)
    for position, parts in cuts:
        draws = jnp.exp(jax.random.uniform(jax.random.fold_in(own, position), (parts,), jnp.float32, low / len(cuts), largest / len(cuts)))
        level = level * jnp.repeat(draws, extent[position] // parts).reshape([-1 if axis == position else 1 for axis in range(len(extent))])
    return level


def cumulative_ranks(amount, lean):
    loads = [(1 << 20) // math.isqrt(standing ** lean) + 1 for standing in range(1, amount + 1)]
    spread = 1 + sum(loads) // (1 << 30)
    return np.cumsum(np.array([max(1, weight // spread) for weight in loads]))


def skewed_ids(rng, extent, count, slope):
    grid = cumulative_ranks(count, slope)
    lot = jax.random.randint(jax.random.fold_in(rng, 1), extent, 0, int(grid[count - 1]))
    grade = jnp.searchsorted(jnp.asarray(grid, jnp.int32), lot, side="right")
    return jax.random.permutation(jax.random.fold_in(rng, 2), count)[grade].astype(jnp.int32)


def normal_values(stream_key, shape, deviation, most, shards=(), kind=jnp.bfloat16):
    level = shard_levels(stream_key, shape, shards, -0.22, 0.18) if shards else 1.0
    values = jax.random.normal(stream_key, shape, jnp.float32) * deviation * level
    return jnp.minimum(jnp.maximum(values, -most), most).astype(kind)


def setup_inputs(seed: int = 0) -> dict:
    key_of = jax.random.split(jax.random.key(seed), 15)
    return {
        "token_ids": with_ends(skewed_ids(key_of[0], (TOTAL,), VOCAB, 2), jax.random.fold_in(key_of[0], 3), 0, VOCAB - 1).astype(jnp.int32),
        "embed_table": normal_values(key_of[1], (VOCAB, D), 1.0, 6.0, ((1, 8),)),
        "se_query": normal_values(key_of[2], (TOTAL, D), 0.5, 3.0, ((0, 32), (1, 8))),
        "se_key": normal_values(key_of[3], (TOTAL, D), 1.0, 6.0, ((0, 32), (1, 8))),
        "se_filter": normal_values(key_of[4], (GROUPS, SE_LEN), SE_LEN ** -0.5, 2.0, ((0, 8),)),
        "mr_query": normal_values(key_of[5], (TOTAL, D), 0.5, 3.0, ((0, 32), (1, 8))),
        "mr_key": normal_values(key_of[6], (TOTAL, D), 1.0, 6.0, ((0, 32), (1, 8))),
        "mr_filter": normal_values(key_of[7], (GROUPS, MR_LEN), MR_LEN ** -0.5, 0.5, ((0, 8),)),
        "li_query": normal_values(key_of[8], (TOTAL, D), 0.5, 3.0, ((0, 32), (1, 8))),
        "li_key": normal_values(key_of[9], (TOTAL, D), 1.0, 6.0, ((0, 32), (1, 8))),
        "li_rate": jnp.clip(jnp.exp(math.log(0.05) - 10.620351 * jax.random.uniform(key_of[10], (GROUPS, STATE), jnp.float32) ** shard_levels(key_of[10], (GROUPS, STATE), ((0, 8),), -0.2, 0.2)), 1.220703097715159e-06, 0.05),
        "li_residue": normal_values(key_of[11], (GROUPS, STATE), 0.25, 1.5, ((0, 8),), jnp.float32),
        "attn_query": draw_attn_query(jax.random.fold_in(key_of[14], 71), 0),
        "attn_key": draw_attn_key(jax.random.fold_in(key_of[14], 71), 0),
    }


def grouped_conv(signal, filters):
    tap_count = filters.shape[1]
    row_total = signal.shape[0]
    tap_weights = jnp.repeat(filters.astype(jnp.float32), GROUP_CH, axis=0)
    padded = jnp.concatenate([jnp.zeros((tap_count - 1, signal.shape[1]), jnp.float32), signal.astype(jnp.float32)], 0)

    def add_tap(tap_index, running):
        start_row = (tap_count - 1 - tap_index).astype(jnp.int32)
        window = lax.dynamic_slice_in_dim(padded, start_row, row_total, 0)
        column = lax.dynamic_index_in_dim(tap_weights, tap_index.astype(jnp.int32), 1, keepdims=False)
        return running + window * column[None, :]
    return lax.fori_loop(0, tap_count, add_tap, jnp.zeros((row_total, signal.shape[1]), jnp.float32))

def gated_layer(stream, out_gate, in_gate, filters):
    gated_in = (in_gate.astype(jnp.float32) * stream.astype(jnp.float32)).astype(jnp.bfloat16)
    conv_out = grouped_conv(gated_in, filters)
    return (stream.astype(jnp.float32) + out_gate.astype(jnp.float32) * conv_out).astype(jnp.bfloat16)

def modal_layer(stream, out_gate, in_gate, li_rate, li_residue):
    gated_in = (in_gate.astype(jnp.float32) * stream.astype(jnp.float32)).astype(jnp.bfloat16)
    gain = li_residue * jnp.sqrt(1.0 - jnp.exp(-2.0 * li_rate) + 1.0 / TOTAL)
    decay_ch = jnp.repeat(jnp.exp(-li_rate), GROUP_CH, axis=0).T
    gain_ch = jnp.repeat(gain, GROUP_CH, axis=0).T

    def advance(state, row_vals):
        state = decay_ch * state + row_vals[None, :]
        return (state, lax.optimization_barrier(jnp.sum(gain_ch * state, axis=0)))
    _, conv_out = lax.scan(advance, jnp.zeros((STATE, D), jnp.float32), gated_in.astype(jnp.float32))
    return (stream.astype(jnp.float32) + out_gate.astype(jnp.float32) * conv_out).astype(jnp.bfloat16)

def reference(token_ids, embed_table, se_query, se_key, se_filter, mr_query, mr_key, mr_filter, li_query, li_key, li_rate, li_residue, attn_query, attn_key):
    stream = embed_table[token_ids]
    stream = gated_layer(stream, se_query, se_key, se_filter)
    stream = gated_layer(stream, mr_query, mr_key, mr_filter)
    stream = modal_layer(stream, li_query, li_key, li_rate, li_residue)
    scale = HEAD_DIM ** (-0.5)
    positions = jnp.arange(TOTAL, dtype=jnp.int32)
    allowed = positions[None, :] <= positions[:, None]
    head_q = attn_query.reshape(TOTAL, HEADS, HEAD_DIM).transpose(1, 0, 2)
    head_k = attn_key.reshape(TOTAL, HEADS, HEAD_DIM).transpose(1, 0, 2)
    head_v = stream.reshape(TOTAL, HEADS, HEAD_DIM).transpose(1, 0, 2)

    def one_head(packed):
        query_h, key_h, value_h = packed
        scores = jnp.dot(query_h.astype(jnp.float32), key_h.astype(jnp.float32).T, precision=lax.Precision.HIGHEST) * scale
        scores = jnp.where(allowed, scores, -1e+30)
        peak = lax.optimization_barrier(jnp.max(scores, axis=1, keepdims=True))
        weights = jnp.where(allowed, jnp.exp(scores - peak), 0.0)
        totals = lax.optimization_barrier(jnp.sum(weights, axis=1))
        weights_low = weights.astype(jnp.bfloat16)
        mixed = jnp.dot(weights_low.astype(jnp.float32), value_h.astype(jnp.float32), precision=lax.Precision.HIGHEST)
        return (mixed / totals[:, None]).astype(jnp.bfloat16)
    attended = lax.map(one_head, (head_q, head_k, head_v))
    attended = attended.transpose(1, 0, 2).reshape(TOTAL, D)
    return (stream.astype(jnp.float32) + attended.astype(jnp.float32)).astype(jnp.bfloat16)
```

```python
import jax
import jax.numpy as jnp
from jax import lax
from jax.experimental import pallas as pl
from jax.experimental.pallas import tpu as pltpu
from jax.sharding import PartitionSpec as P


F32 = jnp.float32
BF16 = jnp.bfloat16
HEAD = 128
LANES = 128
STRIPE = 4
FACTOR = HEAD ** (-0.5) * 1.4426950408889634
MIB = 2**20


def lane_groups(rows, lanes, width):
    return (lax.broadcasted_iota(jnp.int32, (rows, lanes), 1) % LANES) // width


def tables_kernel(mr_ref, rate_ref, res_ref, total_len, mr_out, li_out):
    at = pl.program_id(0)
    groups, taps = mr_ref.shape
    modes = rate_ref.shape[1]
    span = 2 * taps
    k_id = lax.broadcasted_iota(jnp.int32, (taps, span), 0)
    s_id = lax.broadcasted_iota(jnp.int32, (taps, span), 1)
    reverse = (s_id == taps - k_id).astype(BF16)
    first = jnp.dot(mr_ref[...], reverse, preferred_element_type=F32)
    rate = rate_ref[...]
    gain = res_ref[...] * jnp.sqrt(1.0 - jnp.exp(-2.0 * rate) + 1.0 / total_len)
    s_row = lax.broadcasted_iota(jnp.int32, (groups, span), 1)
    lag = jnp.where(s_row <= taps, taps - s_row, taps + span - s_row).astype(F32)
    to_end = (span - 1 - s_row).astype(F32)
    rows = jnp.zeros((groups, span), F32)
    for m in range(modes):
        column = rate[:, m : m + 1]
        rows = rows + gain[:, m : m + 1] * jnp.exp(-column * lag)
        li_out[at, groups * taps + m * groups : groups * taps + (m + 1) * groups, :] = jnp.exp(
            -column * to_end
        ).astype(BF16)
    keep = s_id <= k_id + taps
    for g in range(groups):
        wide = jnp.broadcast_to(first[g : g + 1, :], (taps, span))
        wide = pltpu.roll(wide, 0, 1, stride=1, stride_axis=0)
        mr_out[at, g * taps : (g + 1) * taps, :] = wide.astype(BF16)
        wide = jnp.broadcast_to(rows[g : g + 1, :], (taps, span))
        wide = pltpu.roll(wide, 0, 1, stride=1, stride_axis=0)
        li_out[at, g * taps : (g + 1) * taps, :] = jnp.where(keep, wide, 0.0).astype(BF16)


def make_tables(mr_filter, li_rate, li_residue, total_len):
    group_count, taps = mr_filter.shape
    modes = li_rate.shape[1]
    per = 8
    blocks = group_count // per

    def body(mr_ref, rate_ref, res_ref, mr_out, li_out):
        tables_kernel(mr_ref, rate_ref, res_ref, total_len, mr_out, li_out)

    return pl.pallas_call(
        body,
        grid=(blocks,),
        in_specs=[
            pl.BlockSpec((per, taps), lambda i: (i, 0)),
            pl.BlockSpec((per, modes), lambda i: (i, 0)),
            pl.BlockSpec((per, modes), lambda i: (i, 0)),
        ],
        out_specs=[pl.BlockSpec(memory_space=pltpu.VMEM)] * 2,
        out_shape=[
            pltpu.VMEM((blocks, per * taps, 2 * taps), BF16),
            pltpu.VMEM((blocks, per * (taps + modes), 2 * taps), BF16),
        ],
        compiler_params=pltpu.CompilerParams(vmem_limit_bytes=24 * MIB),
        name="tables",
    )(mr_filter, li_rate, li_residue)


def embed(tok, table):
    ids = lax.broadcasted_iota(jnp.int32, (tok.shape[0], table.shape[0]), 1)
    one_hot = (tok == ids).astype(BF16)
    return jnp.dot(one_hot, table, preferred_element_type=F32)


def edge_kernel(tok_ref, table_ref, key_ref, out_ref):
    out_ref[...] = (key_ref[...].astype(F32) * embed(tok_ref[...], table_ref[...])).astype(BF16)


def se_kernel(tok_ref, table_ref, edge_ref, query_ref, key_ref, filt_ref, next_ref, stream_out, input_out, tail_out):
    emb = embed(tok_ref[...], table_ref[...])
    rows = emb.shape[0]
    gated = (key_ref[...].astype(F32) * emb).astype(BF16).astype(F32)
    edge = edge_ref[...].astype(F32)
    halo = edge.shape[0]
    padded = jnp.concatenate([edge, gated], 0)
    weights = filt_ref[...]
    conv = gated * weights[0:1, :]
    for k in range(1, weights.shape[0]):
        conv = conv + padded[halo - k : halo - k + rows] * weights[k : k + 1, :]
    stream = (emb + query_ref[...].astype(F32) * conv).astype(BF16)
    stream_out[...] = stream
    gated = (next_ref[...].astype(F32) * stream.astype(F32)).astype(BF16)
    input_out[...] = gated
    tail_out[...] = gated[rows - tail_out.shape[0] :]


def fold_groups(res, taps, groups, width):
    lane_group = lane_groups(taps, res.shape[1], width)
    total = res[0:taps]
    for g in range(1, groups):
        total = jnp.where(lane_group == g, res[g * taps : (g + 1) * taps], total)
    return total


def conv_kernel(mr_tab, li_tab, in_ref, halo_ref, stream_ref, mrq_ref, lik_ref, liq_ref, out_ref):
    at = pl.program_id(0)
    taps = halo_ref.shape[0]
    groups = mr_tab.shape[1] // taps
    modes = li_tab.shape[1] // groups - taps
    width = LANES // groups
    near, far = in_ref[0:taps, :], in_ref[taps:, :]
    right = jnp.concatenate([near, far], 0)
    pair = jnp.concatenate([jnp.concatenate([halo_ref[...], near], 0), right], 1)
    res = jnp.dot(mr_tab[at], pair, preferred_element_type=F32)
    both = fold_groups(res, taps, groups, width)
    conv = jnp.concatenate([both[:, :LANES], both[:, LANES:]], 0)
    stream = (stream_ref[...].astype(F32) + mrq_ref[...].astype(F32) * conv).astype(BF16)
    stream_f = stream.astype(F32)
    gated = (lik_ref[...].astype(F32) * stream_f).astype(BF16)
    near = gated[0:taps, :]
    pair = jnp.concatenate([jnp.concatenate([jnp.zeros_like(near), near], 0), gated], 1)
    res = jnp.dot(li_tab[at], pair, preferred_element_type=F32)
    both = fold_groups(res, taps, groups, width)
    conv = jnp.concatenate([both[:, :LANES], both[:, LANES:]], 0)
    rows = conv.shape[0]
    out_ref[0, 0:rows, :] = (stream_f + liq_ref[...].astype(F32) * conv).astype(BF16)
    ends = res[groups * taps :, LANES:].reshape(modes, groups, LANES)
    mine = lax.broadcasted_iota(jnp.int32, (modes, groups, LANES), 2) // width
    mine = mine == lax.broadcasted_iota(jnp.int32, (modes, groups, LANES), 1)
    state = jnp.sum(jnp.where(mine, ends, 0.0), axis=1)
    high = state.astype(BF16)
    out_ref[0, rows : rows + modes, :] = high
    out_ref[0, rows + modes : rows + 2 * modes, :] = (state - high.astype(F32)).astype(BF16)


def pack_kernel(a_ref, b_ref, c_ref, out_ref):
    rows = a_ref.shape[0]
    for j in range(out_ref.shape[0]):
        for n, ref in enumerate((a_ref, b_ref, c_ref)):
            out_ref[j, n * rows : (n + 1) * rows, :] = ref[:, j * HEAD : (j + 1) * HEAD]


def value_kernel(where_ref, pack_ref, all_ref, liq_ref, s1_ref, s2_ref, s3_ref, rate_ref, res_ref,
                 total_len, out_ref, emit, carry):
    i = pl.program_id(0)
    blocks = all_ref.shape[0]
    rows = out_ref.shape[1]
    modes = rate_ref.shape[0]

    @pl.when(i == 0)
    def _():
        x = where_ref[1]
        rate = rate_ref[...]
        gain = res_ref[...] * jnp.sqrt(1.0 - jnp.exp(-2.0 * rate) + 1.0 / total_len)
        step = (lax.broadcasted_iota(jnp.int32, (rows, LANES), 0) + 1).astype(F32)
        for m in range(modes):
            emit[m] = gain[m : m + 1, :] * jnp.exp(-rate[m : m + 1, :] * step)
        decays = [jnp.exp(-rate * (rows * k)) for k in range(STRIPE + 1)]
        scans = []
        for part in (all_ref, s1_ref, s2_ref, s3_ref):
            running = jnp.zeros((modes, LANES), F32)
            seen = [running]
            for b in range(blocks):
                here = part[b, 0:modes, :].astype(F32) + part[b, modes : 2 * modes, :].astype(F32)
                running = running * decays[STRIPE] + here
                seen.append(running)
            scans.append(seen)
        for b in range(blocks):
            total = decays[STRIPE - 1] * scans[0][b]
            for k in range(1, STRIPE):
                total = total + decays[k - 1] * jnp.where(x >= k, scans[k][b + 1], scans[k][b])
            carry[b] = total

    conv = jnp.zeros((rows, LANES), F32)
    for m in range(modes):
        conv = conv + emit[m] * carry[i, m : m + 1, :]
    value = (pack_ref[0].astype(F32) + liq_ref[0].astype(F32) * conv).astype(BF16)
    out_ref[0] = value


def causal(scores, x, k, rows):
    head = scores[:rows]
    if k == 0:
        row = lax.broadcasted_iota(jnp.int32, head.shape, 0)
        col = lax.broadcasted_iota(jnp.int32, head.shape, 1)
        head = jnp.where(col <= row, head, -1e30)
    else:
        head = jnp.where(x >= k, head, -1e30)
    if scores.shape[0] == rows:
        return head
    return jnp.concatenate([head, scores[rows:]], 0)


def products(where_ref, q_ref, refs, use):
    depth, rows, _ = q_ref.shape
    x = where_ref[1]
    for g in range(depth):
        query = q_ref[g:].reshape((depth - g) * rows, HEAD)
        for n, (k, first, ref) in enumerate(refs):
            if first <= g < first + ref.shape[0]:
                scores = lax.dot_general(
                    query, ref[g - first], (((1,), (1,)), ((), ())), preferred_element_type=F32
                )
                use(g, n, causal(scores, x, k, rows))


def peak_kernel(where_ref, q_ref, k0, k1, k2, k3, k4, peak_out, top_ref):
    depth, rows, _ = q_ref.shape
    top_ref[...] = jnp.full(top_ref.shape, -1e30, F32)

    def use(g, n, scores):
        top = jnp.maximum(scores[:, :LANES], scores[:, LANES:])
        top_ref[g * rows :] = jnp.maximum(top_ref[g * rows :], top)

    half = depth // 2
    refs = ((0, 0, k0), (1, 0, k1), (2, 0, k2), (2, half, k3), (3, 0, k4))
    products(where_ref, q_ref, refs, use)
    for i in range(depth):
        part = jnp.max(top_ref[i * rows : (i + 1) * rows], axis=1, keepdims=True)
        peak_out[i * rows : (i + 1) * rows] = jnp.broadcast_to(part * FACTOR, (rows, LANES))


def gather_up(where_ref, q_ref, peak_ref, refs, values, acc_ref, sum_ref):
    rows = q_ref.shape[1]

    def use(g, n, scores):
        shift = peak_ref[g * rows :]
        low = jnp.exp2(scores[:, :LANES] * FACTOR - shift)
        high = jnp.exp2(scores[:, LANES:] * FACTOR - shift)
        sum_ref[g * rows :] = sum_ref[g * rows :] + (low + high)
        weights = jnp.concatenate([low.astype(BF16), high.astype(BF16)], 1)
        value = values[n][g - refs[n][1]]
        mixed = jnp.dot(weights, value, preferred_element_type=F32)
        acc_ref[g * rows :] = acc_ref[g * rows :] + mixed

    products(where_ref, q_ref, refs, use)


def near_kernel(where_ref, q_ref, peak_ref, k0, k1, k4, v0, v1, v4, acc_ref, sum_ref):
    acc_ref[...] = jnp.zeros(acc_ref.shape, F32)
    sum_ref[...] = jnp.zeros(sum_ref.shape, F32)
    refs = ((0, 0, k0), (1, 0, k1), (3, 0, k4))
    gather_up(where_ref, q_ref, peak_ref, refs, (v0, v1, v4), acc_ref, sum_ref)


def far_kernel(where_ref, q_ref, peak_ref, k2, k3, v2, v3, v0, acc_in, sum_in, out_ref, acc_ref, sum_ref):
    depth, rows, _ = q_ref.shape
    acc_ref[...] = acc_in[...]
    sum_ref[...] = sum_in[...]
    refs = ((2, 0, k2), (2, depth // 2, k3))
    gather_up(where_ref, q_ref, peak_ref, refs, (v2, v3), acc_ref, sum_ref)
    for i in range(depth):
        place = slice(i * rows, (i + 1) * rows)
        total = jnp.sum(sum_ref[place], axis=1, keepdims=True)
        attended = (acc_ref[place] / total).astype(BF16)
        out_ref[i] = (v0[i].astype(F32) + attended.astype(F32)).astype(BF16)


def whole(shape):
    return pl.BlockSpec(shape, lambda *_: (0,) * len(shape))


def local(
    token_ids,
    embed_table,
    se_query,
    se_key,
    se_filter,
    mr_query,
    mr_key,
    mr_filter,
    li_query,
    li_key,
    li_rate,
    li_residue,
    attn_query,
    attn_key,
):
    rows = token_ids.shape[0]
    vocab, channels = embed_table.shape
    group_count = se_filter.shape[0]
    width = channels // group_count
    seq = lax.axis_size("seq")
    total_len = rows * seq
    heads = channels // HEAD
    depth = seq // STRIPE
    taps = mr_filter.shape[1]
    modes = li_rate.shape[1]
    here = lax.axis_index("seq")
    where = jnp.stack([here // STRIPE, here % STRIPE]).astype(jnp.int32)
    smem = pl.BlockSpec(memory_space=pltpu.SMEM)
    columns = [[z * STRIPE + x for z in range(depth)] for x in range(STRIPE)]
    forward = [(d, d + 1) for d in range(seq - 1)]

    def turn(shift):
        return [(d, d // STRIPE * STRIPE + (d + shift) % STRIPE) for d in range(seq)]

    def exchange(packed):
        return lax.all_to_all(
            packed, "seq", split_axis=0, concat_axis=0, tiled=True, axis_index_groups=columns
        )

    def spread(part):
        behind = lax.ppermute(part, "seq", turn(1))
        ahead = lax.ppermute(part, "seq", turn(STRIPE - 1))
        half = depth // 2
        across = [
            lax.ppermute(behind[:half], "seq", turn(1)),
            lax.ppermute(ahead[half:], "seq", turn(STRIPE - 1)),
        ]
        return part, behind, *across, ahead

    early = pl.pallas_call(
        pack_kernel,
        grid=(2,),
        in_specs=[pl.BlockSpec((rows, channels // 2), lambda j: (0, j))] * 3,
        out_specs=pl.BlockSpec((heads // 2, 3 * rows, HEAD), lambda j: (j, 0, 0)),
        out_shape=jax.ShapeDtypeStruct((heads, 3 * rows, HEAD), BF16),
        name="pack",
    )(attn_query, attn_key, li_query)

    tok = token_ids[:, None]
    halo = 8
    last = rows // halo - 1
    edge = pl.pallas_call(
        edge_kernel,
        grid=(1,),
        in_specs=[
            pl.BlockSpec((halo, 1), lambda i: (last, 0)),
            whole((vocab, channels)),
            pl.BlockSpec((halo, channels), lambda i: (last, 0)),
        ],
        out_specs=whole((halo, channels)),
        out_shape=jax.ShapeDtypeStruct((halo, channels), BF16),
        name="edge",
    )(tok, embed_table, se_key)
    edge = lax.ppermute(edge, "seq", forward)

    mr_tab, li_tab = make_tables(mr_filter, li_rate, li_residue, total_len)

    se_taps = se_filter.shape[1]
    se_weights = jnp.broadcast_to(
        se_filter.astype(F32).T[:, :, None], (se_taps, group_count, width)
    ).reshape(se_taps, channels)
    wide = 256
    column = pl.BlockSpec((rows, wide), lambda j: (0, j))
    stream, mr_input, mr_tail = pl.pallas_call(
        se_kernel,
        grid=(channels // wide,),
        in_specs=[
            whole((rows, 1)),
            pl.BlockSpec((vocab, wide), lambda j: (0, j)),
            pl.BlockSpec((halo, wide), lambda j: (0, j)),
            column,
            column,
            pl.BlockSpec((se_taps, wide), lambda j: (0, j)),
            column,
        ],
        out_specs=[column, column, pl.BlockSpec((taps, wide), lambda j: (0, j))],
        out_shape=[jax.ShapeDtypeStruct((rows, channels), BF16)] * 2
        + [jax.ShapeDtypeStruct((taps, channels), BF16)],
        name="short",
    )(tok, embed_table, edge, se_query, se_key, se_weights, mr_key)
    mr_edge = lax.ppermute(mr_tail, "seq", forward)
    early, mr_input = lax.optimization_barrier((early, mr_input))
    early = exchange(early)

    column = pl.BlockSpec((rows, LANES), lambda j: (0, j))
    packed = pl.pallas_call(
        conv_kernel,
        grid=(heads,),
        in_specs=[
            pl.BlockSpec(memory_space=pltpu.VMEM),
            pl.BlockSpec(memory_space=pltpu.VMEM),
            column,
            pl.BlockSpec((taps, LANES), lambda j: (0, j)),
            column,
            column,
            column,
            column,
        ],
        out_specs=pl.BlockSpec((1, rows + 2 * modes, LANES), lambda j: (j, 0, 0)),
        out_shape=jax.ShapeDtypeStruct((heads, rows + 2 * modes, LANES), BF16),
        compiler_params=pltpu.CompilerParams(vmem_limit_bytes=24 * MIB),
        name="medium_long",
    )(mr_tab, li_tab, mr_input, mr_edge, stream, mr_query, li_key, li_query)
    packed = exchange(packed)

    query = early[:, :rows]
    keys = spread(early[:, rows : 2 * rows])
    states = packed[:, rows:]
    others = [lax.ppermute(states, "seq", turn(k)) for k in range(1, STRIPE)]

    def per_channel(value):
        value = jnp.broadcast_to(value.T[:, :, None], (modes, group_count, width))
        return value.reshape(modes, channels)

    def mine(value):
        return lax.dynamic_slice_in_dim(per_channel(value), where[0] * HEAD, HEAD, axis=1)

    def value_body(*refs):
        value_kernel(*refs[:9], total_len, *refs[9:])

    state_spec = whole((depth, 2 * modes, LANES))
    block = pl.BlockSpec((1, rows, LANES), lambda i: (i, 0, 0))
    values = pl.pallas_call(
        value_body,
        grid=(depth,),
        in_specs=[
            smem,
            block,
            state_spec,
            pl.BlockSpec((1, rows, LANES), lambda i: (i, 2, 0)),
            state_spec,
            state_spec,
            state_spec,
            whole((modes, LANES)),
            whole((modes, LANES)),
        ],
        out_specs=block,
        out_shape=jax.ShapeDtypeStruct((depth, rows, LANES), BF16),
        scratch_shapes=[
            pltpu.VMEM((modes, rows, LANES), F32),
            pltpu.VMEM((depth, modes, LANES), F32),
        ],
        name="values",
    )(where, packed, states, early, *others, mine(li_rate), mine(li_residue))
    values = spread(values)

    inside = pl.BlockSpec(memory_space=pltpu.VMEM)
    reach = depth * rows
    peaks = pl.pallas_call(
        peak_kernel,
        in_specs=[smem] + [inside] * 6,
        out_specs=inside,
        out_shape=jax.ShapeDtypeStruct((reach, LANES), F32),
        scratch_shapes=[pltpu.VMEM((reach, LANES), F32)],
        compiler_params=pltpu.CompilerParams(vmem_limit_bytes=30 * MIB),
        name="peaks",
    )(where, query, *keys)
    k0, k1, k2, k3, k4 = keys
    v0, v1, v2, v3, v4 = values
    sums = jax.ShapeDtypeStruct((reach, LANES), F32)
    near = pl.pallas_call(
        near_kernel,
        in_specs=[smem] + [inside] * 8,
        out_specs=[inside, inside],
        out_shape=[sums, sums],
        compiler_params=pltpu.CompilerParams(vmem_limit_bytes=40 * MIB),
        name="near",
    )(where, query, peaks, k0, k1, k4, v0, v1, v4)
    result = pl.pallas_call(
        far_kernel,
        in_specs=[smem] + [inside] * 9,
        out_specs=inside,
        out_shape=jax.ShapeDtypeStruct((depth, rows, HEAD), BF16),
        scratch_shapes=[pltpu.VMEM((reach, HEAD), F32), pltpu.VMEM((reach, LANES), F32)],
        compiler_params=pltpu.CompilerParams(vmem_limit_bytes=40 * MIB),
        name="far",
    )(where, query, peaks, k2, k3, v2, v3, v0, *near)
    result = exchange(result)
    return result.transpose(1, 0, 2).reshape(rows, channels)


def solution(mesh):
    wide = P("seq", "chan")
    narrow = P("chan", None)
    in_specs = (
        P("seq"), P(None, "chan"), wide, wide, narrow, wide, wide, narrow, wide, wide, narrow,
        narrow, wide, wide,
    )

    return jax.shard_map(local, mesh=mesh, in_specs=in_specs, out_specs=wide, check_vma=False)
```

```python
import jax
import jax.numpy as jnp
from jax import lax
from jax.experimental import pallas as pl
from jax.experimental.pallas import tpu as pltpu
from jax.sharding import PartitionSpec as P


F32 = jnp.float32
BF16 = jnp.bfloat16
HEAD = 128
LANES = 128
STRIPE = 4
FACTOR = HEAD ** (-0.5) * 1.4426950408889634
MIB = 2**20


def lane_groups(rows, lanes, width):
    return (lax.broadcasted_iota(jnp.int32, (rows, lanes), 1) % LANES) // width


def tables_kernel(mr_ref, rate_ref, res_ref, total_len, mr_out, li_out):
    at = pl.program_id(0)
    groups, taps = mr_ref.shape
    modes = rate_ref.shape[1]
    span = 2 * taps
    k_id = lax.broadcasted_iota(jnp.int32, (taps, span), 0)
    s_id = lax.broadcasted_iota(jnp.int32, (taps, span), 1)
    reverse = (s_id == taps - k_id).astype(BF16)
    first = jnp.dot(mr_ref[...], reverse, preferred_element_type=F32)
    rate = rate_ref[...]
    gain = res_ref[...] * jnp.sqrt(1.0 - jnp.exp(-2.0 * rate) + 1.0 / total_len)
    s_row = lax.broadcasted_iota(jnp.int32, (groups, span), 1)
    lag = jnp.where(s_row <= taps, taps - s_row, taps + span - s_row).astype(F32)
    to_end = (span - 1 - s_row).astype(F32)
    rows = jnp.zeros((groups, span), F32)
    for m in range(modes):
        column = rate[:, m : m + 1]
        rows = rows + gain[:, m : m + 1] * jnp.exp(-column * lag)
        li_out[at, groups * taps + m * groups : groups * taps + (m + 1) * groups, :] = jnp.exp(
            -column * to_end
        ).astype(BF16)
    keep = s_id <= k_id + taps
    for g in range(groups):
        wide = jnp.broadcast_to(first[g : g + 1, :], (taps, span))
        wide = pltpu.roll(wide, 0, 1, stride=1, stride_axis=0)
        mr_out[at, g * taps : (g + 1) * taps, :] = wide.astype(BF16)
        wide = jnp.broadcast_to(rows[g : g + 1, :], (taps, span))
        wide = pltpu.roll(wide, 0, 1, stride=1, stride_axis=0)
        li_out[at, g * taps : (g + 1) * taps, :] = jnp.where(keep, wide, 0.0).astype(BF16)


def make_tables(mr_filter, li_rate, li_residue, total_len):
    group_count, taps = mr_filter.shape
    modes = li_rate.shape[1]
    per = 8
    blocks = group_count // per

    def body(mr_ref, rate_ref, res_ref, mr_out, li_out):
        tables_kernel(mr_ref, rate_ref, res_ref, total_len, mr_out, li_out)

    return pl.pallas_call(
        body,
        grid=(blocks,),
        in_specs=[
            pl.BlockSpec((per, taps), lambda i: (i, 0)),
            pl.BlockSpec((per, modes), lambda i: (i, 0)),
            pl.BlockSpec((per, modes), lambda i: (i, 0)),
        ],
        out_specs=[pl.BlockSpec(memory_space=pltpu.VMEM)] * 2,
        out_shape=[
            pltpu.VMEM((blocks, per * taps, 2 * taps), BF16),
            pltpu.VMEM((blocks, per * (taps + modes), 2 * taps), BF16),
        ],
        compiler_params=pltpu.CompilerParams(vmem_limit_bytes=24 * MIB),
        name="tables",
    )(mr_filter, li_rate, li_residue)


def embed(tok, table):
    ids = lax.broadcasted_iota(jnp.int32, (tok.shape[0], table.shape[0]), 1)
    one_hot = (tok == ids).astype(BF16)
    return jnp.dot(one_hot, table, preferred_element_type=F32)


def edge_kernel(tok_ref, table_ref, key_ref, out_ref):
    out_ref[...] = (key_ref[...].astype(F32) * embed(tok_ref[...], table_ref[...])).astype(BF16)


def se_kernel(tok_ref, table_ref, edge_ref, query_ref, key_ref, filt_ref, next_ref, stream_out, input_out, tail_out):
    emb = embed(tok_ref[...], table_ref[...])
    rows = emb.shape[0]
    gated = (key_ref[...].astype(F32) * emb).astype(BF16).astype(F32)
    edge = edge_ref[...].astype(F32)
    halo = edge.shape[0]
    padded = jnp.concatenate([edge, gated], 0)
    weights = filt_ref[...]
    conv = gated * weights[0:1, :]
    for k in range(1, weights.shape[0]):
        conv = conv + padded[halo - k : halo - k + rows] * weights[k : k + 1, :]
    stream = (emb + query_ref[...].astype(F32) * conv).astype(BF16)
    stream_out[...] = stream
    gated = (next_ref[...].astype(F32) * stream.astype(F32)).astype(BF16)
    input_out[...] = gated
    tail_out[...] = gated[rows - tail_out.shape[0] :]


def fold_groups(res, taps, groups, width):
    lane_group = lane_groups(taps, res.shape[1], width)
    total = res[0:taps]
    for g in range(1, groups):
        total = jnp.where(lane_group == g, res[g * taps : (g + 1) * taps], total)
    return total


def conv_kernel(where_ref, mr_tab, li_tab, in_ref, halo_ref, stream_ref, mrq_ref, lik_ref, liq_ref, *outs):
    step = pl.program_id(0)
    at = lax.rem(where_ref[0] + step, len(outs))
    taps = halo_ref.shape[0]
    groups = mr_tab.shape[1] // taps
    modes = li_tab.shape[1] // groups - taps
    width = LANES // groups
    near, far = in_ref[0:taps, :], in_ref[taps:, :]
    right = jnp.concatenate([near, far], 0)
    pair = jnp.concatenate([jnp.concatenate([halo_ref[...], near], 0), right], 1)
    res = jnp.dot(mr_tab[at], pair, preferred_element_type=F32)
    both = fold_groups(res, taps, groups, width)
    conv = jnp.concatenate([both[:, :LANES], both[:, LANES:]], 0)
    stream = (stream_ref[...].astype(F32) + mrq_ref[...].astype(F32) * conv).astype(BF16)
    stream_f = stream.astype(F32)
    gated = (lik_ref[...].astype(F32) * stream_f).astype(BF16)
    near = gated[0:taps, :]
    pair = jnp.concatenate([jnp.concatenate([jnp.zeros_like(near), near], 0), gated], 1)
    res = jnp.dot(li_tab[at], pair, preferred_element_type=F32)
    both = fold_groups(res, taps, groups, width)
    conv = jnp.concatenate([both[:, :LANES], both[:, LANES:]], 0)
    rows = conv.shape[0]
    wide = (stream_f + liq_ref[...].astype(F32) * conv).astype(BF16)
    ends = res[groups * taps :, LANES:].reshape(modes, groups, LANES)
    mine = lax.broadcasted_iota(jnp.int32, (modes, groups, LANES), 2) // width
    mine = mine == lax.broadcasted_iota(jnp.int32, (modes, groups, LANES), 1)
    state = jnp.sum(jnp.where(mine, ends, 0.0), axis=1)
    high = state.astype(BF16)
    low = (state - high.astype(F32)).astype(BF16)
    for s, out_ref in enumerate(outs):

        @pl.when(step == s)
        def _():
            out_ref[0:rows, :] = wide
            out_ref[rows : rows + modes, :] = high
            out_ref[rows + modes : rows + 2 * modes, :] = low


def pack_kernel(a_ref, b_ref, c_ref, out_ref):
    rows = a_ref.shape[0]
    for j in range(out_ref.shape[0]):
        for n, ref in enumerate((a_ref, b_ref, c_ref)):
            out_ref[j, n * rows : (n + 1) * rows, :] = ref[:, j * HEAD : (j + 1) * HEAD]


def unpack(where, parts, cuts):
    count = len(parts)
    bounds = list(zip((0,) + cuts[:-1], cuts))
    parts = [part.reshape(cuts[-1], LANES) for part in parts]

    def body(where_ref, *refs):
        for s in range(count):
            z = lax.rem(where_ref[0] + count - s, count)
            for (low, high), out_ref in zip(bounds, refs[count:]):
                out_ref[z] = refs[s][low:high, :]

    inside = pl.BlockSpec(memory_space=pltpu.VMEM)
    return pl.pallas_call(
        body,
        in_specs=[pl.BlockSpec(memory_space=pltpu.SMEM)] + [inside] * count,
        out_specs=[inside] * len(cuts),
        out_shape=[jax.ShapeDtypeStruct((count, high - low, LANES), BF16) for low, high in bounds],
        compiler_params=pltpu.CompilerParams(vmem_limit_bytes=16 * MIB),
    )(where, *parts)


def value_kernel(where_ref, pack_ref, all_ref, liq_ref, s1_ref, s2_ref, s3_ref, rate_ref, res_ref,
                 total_len, out_ref, emit):
    blocks, rows, _ = out_ref.shape
    modes = rate_ref.shape[0]
    x = where_ref[1]
    rate = rate_ref[...]
    step = (lax.broadcasted_iota(jnp.int32, (rows, LANES), 0) + 1).astype(F32)

    @pl.loop(0, modes)
    def _(m):
        slow, strength = rate_ref[pl.ds(m, 1), :], res_ref[pl.ds(m, 1), :]
        strength = strength * jnp.sqrt(1.0 - jnp.exp(-2.0 * slow) + 1.0 / total_len)
        emit[m] = strength * jnp.exp(-slow * step)

    decays = [jnp.exp(-rate * (rows * k)) for k in range(STRIPE + 1)]
    scans = []
    for part in (all_ref, s1_ref, s2_ref, s3_ref):
        running = jnp.zeros((modes, LANES), F32)
        seen = [running]
        for b in range(blocks):
            here = part[b, 0:modes, :].astype(F32) + part[b, modes : 2 * modes, :].astype(F32)
            running = running * decays[STRIPE] + here
            seen.append(running)
        scans.append(seen)
    carries = []
    for b in range(blocks):
        total = decays[STRIPE - 1] * scans[0][b]
        for k in range(1, STRIPE):
            total = total + decays[k - 1] * jnp.where(x >= k, scans[k][b + 1], scans[k][b])
        carries.append(total)
    piece = 32

    @pl.loop(0, rows // piece)
    def _(r):
        place = pl.ds(pl.multiple_of(r * piece, piece), piece)
        convs = [jnp.zeros((piece, LANES), F32)] * blocks
        for m in range(modes):
            table = emit[m, place, :]
            convs = [conv + table * carries[b][m : m + 1, :] for b, conv in enumerate(convs)]
        for b, conv in enumerate(convs):
            out_ref[b, place, :] = (
                pack_ref[b, place, :].astype(F32) + liq_ref[b, place, :].astype(F32) * conv
            ).astype(BF16)


def causal(scores, x, k, rows):
    head = scores[:rows]
    if k == 0:
        row = lax.broadcasted_iota(jnp.int32, head.shape, 0)
        col = lax.broadcasted_iota(jnp.int32, head.shape, 1)
        head = jnp.where(col <= row, head, -1e30)
    else:
        head = jnp.where(x >= k, head, -1e30)
    if scores.shape[0] == rows:
        return head
    return jnp.concatenate([head, scores[rows:]], 0)


def products(where_ref, q_ref, refs, use):
    depth, rows, _ = q_ref.shape
    x = where_ref[1]
    for g in range(depth):
        query = q_ref[g:].reshape((depth - g) * rows, HEAD)
        for n, (k, first, ref) in enumerate(refs):
            if first <= g < first + ref.shape[0]:
                scores = lax.dot_general(
                    query, ref[g - first], (((1,), (1,)), ((), ())), preferred_element_type=F32
                )
                use(g, n, causal(scores, x, k, rows))


def peak_kernel(where_ref, q_ref, k0, k1, k2, k3, k4, peak_out, top_ref):
    depth, rows, _ = q_ref.shape
    top_ref[...] = jnp.full(top_ref.shape, -1e30, F32)

    def use(g, n, scores):
        top = jnp.maximum(scores[:, :LANES], scores[:, LANES:])
        top_ref[g * rows :] = jnp.maximum(top_ref[g * rows :], top)

    half = depth // 2
    refs = ((0, 0, k0), (1, 0, k1), (2, 0, k2), (2, half, k3), (3, 0, k4))
    products(where_ref, q_ref, refs, use)
    for i in range(depth):
        part = jnp.max(top_ref[i * rows : (i + 1) * rows], axis=1, keepdims=True)
        peak_out[i * rows : (i + 1) * rows] = jnp.broadcast_to(part * FACTOR, (rows, LANES))


def gather_up(where_ref, q_ref, peak_ref, refs, values, acc_ref, sum_ref):
    rows = q_ref.shape[1]

    def use(g, n, scores):
        shift = peak_ref[g * rows :]
        low = jnp.exp2(scores[:, :LANES] * FACTOR - shift)
        high = jnp.exp2(scores[:, LANES:] * FACTOR - shift)
        sum_ref[g * rows :] = sum_ref[g * rows :] + (low + high)
        weights = jnp.concatenate([low.astype(BF16), high.astype(BF16)], 1)
        value = values[n][g - refs[n][1]]
        mixed = jnp.dot(weights, value, preferred_element_type=F32)
        acc_ref[g * rows :] = acc_ref[g * rows :] + mixed

    products(where_ref, q_ref, refs, use)


def near_kernel(where_ref, q_ref, peak_ref, k0, k1, k4, v0, v1, v4, acc_ref, sum_ref):
    acc_ref[...] = jnp.zeros(acc_ref.shape, F32)
    sum_ref[...] = jnp.zeros(sum_ref.shape, F32)
    refs = ((0, 0, k0), (1, 0, k1), (3, 0, k4))
    gather_up(where_ref, q_ref, peak_ref, refs, (v0, v1, v4), acc_ref, sum_ref)


def far_kernel(where_ref, q_ref, peak_ref, k2, k3, v2, v3, v0, acc_in, sum_in, out_ref, acc_ref, sum_ref):
    depth, rows, _ = q_ref.shape
    acc_ref[...] = acc_in[...]
    sum_ref[...] = sum_in[...]
    refs = ((2, 0, k2), (2, depth // 2, k3))
    gather_up(where_ref, q_ref, peak_ref, refs, (v2, v3), acc_ref, sum_ref)
    for i in range(depth):
        place = slice(i * rows, (i + 1) * rows)
        total = jnp.sum(sum_ref[place], axis=1, keepdims=True)
        attended = (acc_ref[place] / total).astype(BF16)
        out_ref[i] = (v0[i].astype(F32) + attended.astype(F32)).astype(BF16)


def whole(shape):
    return pl.BlockSpec(shape, lambda *_: (0,) * len(shape))


def local(
    token_ids,
    embed_table,
    se_query,
    se_key,
    se_filter,
    mr_query,
    mr_key,
    mr_filter,
    li_query,
    li_key,
    li_rate,
    li_residue,
    attn_query,
    attn_key,
):
    rows = token_ids.shape[0]
    vocab, channels = embed_table.shape
    group_count = se_filter.shape[0]
    width = channels // group_count
    seq = lax.axis_size("seq")
    total_len = rows * seq
    heads = channels // HEAD
    depth = seq // STRIPE
    taps = mr_filter.shape[1]
    modes = li_rate.shape[1]
    here = lax.axis_index("seq")
    where = jnp.stack([here // STRIPE, here % STRIPE]).astype(jnp.int32)
    smem = pl.BlockSpec(memory_space=pltpu.SMEM)
    columns = [[z * STRIPE + x for z in range(depth)] for x in range(STRIPE)]
    forward = [(d, d + 1) for d in range(seq - 1)]

    def turn(shift):
        return [(d, d // STRIPE * STRIPE + (d + shift) % STRIPE) for d in range(seq)]

    def exchange(packed):
        return lax.all_to_all(
            packed, "seq", split_axis=0, concat_axis=0, tiled=True, axis_index_groups=columns
        )

    def shifted(parts):
        return [parts[0]] + [
            lax.ppermute(
                part, "seq", [(d, (d // STRIPE + s) % depth * STRIPE + d % STRIPE) for d in range(seq)]
            )
            for s, part in enumerate(parts)
            if s
        ]

    def spread(part):
        behind = lax.ppermute(part, "seq", turn(1))
        ahead = lax.ppermute(part, "seq", turn(STRIPE - 1))
        half = depth // 2
        across = [
            lax.ppermute(behind[:half], "seq", turn(1)),
            lax.ppermute(ahead[half:], "seq", turn(STRIPE - 1)),
        ]
        return part, behind, *across, ahead

    inside = pl.BlockSpec(memory_space=pltpu.VMEM)
    small = pltpu.CompilerParams(vmem_limit_bytes=16 * MIB)
    early = pl.pallas_call(
        pack_kernel,
        grid=(2,),
        in_specs=[pl.BlockSpec((rows, channels // 2), lambda j: (0, j))] * 3,
        out_specs=pl.BlockSpec((heads // 2, 3 * rows, HEAD), lambda j: (j, 0, 0)),
        out_shape=jax.ShapeDtypeStruct((heads, 3 * rows, HEAD), BF16),
        name="pack",
    )(attn_query, attn_key, li_query)

    tok = token_ids[:, None]
    halo = 8
    last = rows // halo - 1
    edge = pl.pallas_call(
        edge_kernel,
        grid=(1,),
        in_specs=[
            pl.BlockSpec((halo, 1), lambda i: (last, 0)),
            whole((vocab, channels)),
            pl.BlockSpec((halo, channels), lambda i: (last, 0)),
        ],
        out_specs=whole((halo, channels)),
        out_shape=jax.ShapeDtypeStruct((halo, channels), BF16),
        name="edge",
    )(tok, embed_table, se_key)
    edge = lax.ppermute(edge, "seq", forward)

    mr_tab, li_tab = make_tables(mr_filter, li_rate, li_residue, total_len)

    se_taps = se_filter.shape[1]
    se_weights = jnp.broadcast_to(
        se_filter.astype(F32).T[:, :, None], (se_taps, group_count, width)
    ).reshape(se_taps, channels)
    wide = 256
    column = pl.BlockSpec((rows, wide), lambda j: (0, j))
    stream, mr_input, mr_tail = pl.pallas_call(
        se_kernel,
        grid=(channels // wide,),
        in_specs=[
            whole((rows, 1)),
            pl.BlockSpec((vocab, wide), lambda j: (0, j)),
            pl.BlockSpec((halo, wide), lambda j: (0, j)),
            column,
            column,
            pl.BlockSpec((se_taps, wide), lambda j: (0, j)),
            column,
        ],
        out_specs=[column, column, pl.BlockSpec((taps, wide), lambda j: (0, j))],
        out_shape=[jax.ShapeDtypeStruct((rows, channels), BF16)] * 2
        + [jax.ShapeDtypeStruct((taps, channels), BF16)],
        name="short",
    )(tok, embed_table, edge, se_query, se_key, se_weights, mr_key)
    mr_edge = lax.ppermute(mr_tail, "seq", forward)
    early = exchange(early)

    column = pl.BlockSpec((rows, LANES), lambda j, w: (0, lax.rem(w[0] + j, heads)))
    ends = pl.BlockSpec((taps, LANES), lambda j, w: (0, lax.rem(w[0] + j, heads)))
    size = (rows + 2 * modes, LANES)
    packed = pl.pallas_call(
        conv_kernel,
        grid_spec=pltpu.PrefetchScalarGridSpec(
            num_scalar_prefetch=1,
            grid=(heads,),
            in_specs=[inside, inside, column, ends, column, column, column, column],
            out_specs=[pl.BlockSpec(size, lambda j, w: (0, 0))] * heads,
        ),
        out_shape=[jax.ShapeDtypeStruct(size, BF16)] * heads,
        compiler_params=pltpu.CompilerParams(vmem_limit_bytes=24 * MIB),
        name="medium_long",
    )(where, mr_tab, li_tab, mr_input, mr_edge, stream, mr_query, li_key, li_query)
    packed = shifted(packed)

    query, key, early_gate = (early[:, n * rows : (n + 1) * rows] for n in range(3))
    keys = spread(key)
    packed, states = unpack(where, packed, (rows, rows + 2 * modes))
    others = [lax.ppermute(states, "seq", turn(k)) for k in range(1, STRIPE)]

    def mine(value):
        count = HEAD // width
        value = lax.dynamic_slice_in_dim(value, where[0] * count, count, axis=0)
        value = jnp.broadcast_to(value.T[:, :, None], (modes, count, width))
        return value.reshape(modes, HEAD)

    def value_body(*refs):
        value_kernel(*refs[:9], total_len, *refs[9:])

    values = pl.pallas_call(
        value_body,
        in_specs=[smem] + [inside] * 8,
        out_specs=inside,
        out_shape=jax.ShapeDtypeStruct((depth, rows, LANES), BF16),
        scratch_shapes=[pltpu.VMEM((modes, rows, LANES), F32)],
        compiler_params=small,
        name="values",
    )(where, packed, states, early_gate, *others, mine(li_rate), mine(li_residue))
    values = spread(values)

    reach = depth * rows
    peaks = pl.pallas_call(
        peak_kernel,
        in_specs=[smem] + [inside] * 6,
        out_specs=inside,
        out_shape=jax.ShapeDtypeStruct((reach, LANES), F32),
        scratch_shapes=[pltpu.VMEM((reach, LANES), F32)],
        compiler_params=pltpu.CompilerParams(vmem_limit_bytes=30 * MIB),
        name="peaks",
    )(where, query, *keys)
    k0, k1, k2, k3, k4 = keys
    v0, v1, v2, v3, v4 = values
    sums = jax.ShapeDtypeStruct((reach, LANES), F32)
    near = pl.pallas_call(
        near_kernel,
        in_specs=[smem] + [inside] * 8,
        out_specs=[inside, inside],
        out_shape=[sums, sums],
        compiler_params=pltpu.CompilerParams(vmem_limit_bytes=40 * MIB),
        name="near",
    )(where, query, peaks, k0, k1, k4, v0, v1, v4)
    result = pl.pallas_call(
        far_kernel,
        in_specs=[smem] + [inside] * 9,
        out_specs=inside,
        out_shape=jax.ShapeDtypeStruct((depth, rows, HEAD), BF16),
        scratch_shapes=[pltpu.VMEM((reach, HEAD), F32), pltpu.VMEM((reach, LANES), F32)],
        compiler_params=pltpu.CompilerParams(vmem_limit_bytes=40 * MIB),
        name="far",
    )(where, query, peaks, k2, k3, v2, v3, v0, *near)
    result = exchange(result)
    return result.transpose(1, 0, 2).reshape(rows, channels)


def solution(mesh):
    wide = P("seq", "chan")
    narrow = P("chan", None)
    in_specs = (
        P("seq"), P(None, "chan"), wide, wide, narrow, wide, wide, narrow, wide, wide, narrow,
        narrow, wide, wide,
    )

    return jax.shard_map(local, mesh=mesh, in_specs=in_specs, out_specs=wide, check_vma=False)
```

```python
import jax
import jax.numpy as jnp
from jax import lax
from jax.experimental import pallas as pl
from jax.experimental.pallas import tpu as pltpu
from jax.sharding import PartitionSpec as P


F32 = jnp.float32
BF16 = jnp.bfloat16
HEAD = 128
LANES = 128
STRIPE = 4
FACTOR = HEAD ** (-0.5) * 1.4426950408889634
MIB = 2**20


def lane_groups(rows, lanes, width):
    return (lax.broadcasted_iota(jnp.int32, (rows, lanes), 1) % LANES) // width


def tables_kernel(mr_ref, rate_ref, res_ref, total_len, mr_out, li_out):
    at = pl.program_id(0)
    groups, taps = mr_ref.shape
    modes = rate_ref.shape[1]
    span = 2 * taps
    k_id = lax.broadcasted_iota(jnp.int32, (taps, span), 0)
    s_id = lax.broadcasted_iota(jnp.int32, (taps, span), 1)
    reverse = (s_id == taps - k_id).astype(BF16)
    first = jnp.dot(mr_ref[...], reverse, preferred_element_type=F32)
    rate = rate_ref[...]
    gain = res_ref[...] * jnp.sqrt(1.0 - jnp.exp(-2.0 * rate) + 1.0 / total_len)
    s_row = lax.broadcasted_iota(jnp.int32, (groups, span), 1)
    lag = jnp.where(s_row <= taps, taps - s_row, taps + span - s_row).astype(F32)
    to_end = (span - 1 - s_row).astype(F32)
    rows = jnp.zeros((groups, span), F32)
    for m in range(modes):
        column = rate[:, m : m + 1]
        rows = rows + gain[:, m : m + 1] * jnp.exp(-column * lag)
        li_out[at, groups * taps + m * groups : groups * taps + (m + 1) * groups, :] = jnp.exp(
            -column * to_end
        ).astype(BF16)
    keep = s_id <= k_id + taps
    for g in range(groups):
        wide = jnp.broadcast_to(first[g : g + 1, :], (taps, span))
        wide = pltpu.roll(wide, 0, 1, stride=1, stride_axis=0)
        mr_out[at, g * taps : (g + 1) * taps, :] = wide.astype(BF16)
        wide = jnp.broadcast_to(rows[g : g + 1, :], (taps, span))
        wide = pltpu.roll(wide, 0, 1, stride=1, stride_axis=0)
        li_out[at, g * taps : (g + 1) * taps, :] = jnp.where(keep, wide, 0.0).astype(BF16)


def make_tables(mr_filter, li_rate, li_residue, total_len):
    group_count, taps = mr_filter.shape
    modes = li_rate.shape[1]
    per = 8
    blocks = group_count // per

    def body(mr_ref, rate_ref, res_ref, mr_out, li_out):
        tables_kernel(mr_ref, rate_ref, res_ref, total_len, mr_out, li_out)

    return pl.pallas_call(
        body,
        grid=(blocks,),
        in_specs=[
            pl.BlockSpec((per, taps), lambda i: (i, 0)),
            pl.BlockSpec((per, modes), lambda i: (i, 0)),
            pl.BlockSpec((per, modes), lambda i: (i, 0)),
        ],
        out_specs=[pl.BlockSpec(memory_space=pltpu.VMEM)] * 2,
        out_shape=[
            pltpu.VMEM((blocks, per * taps, 2 * taps), BF16),
            pltpu.VMEM((blocks, per * (taps + modes), 2 * taps), BF16),
        ],
        compiler_params=pltpu.CompilerParams(vmem_limit_bytes=24 * MIB),
        name="tables",
    )(mr_filter, li_rate, li_residue)


def embed(tok, table):
    ids = lax.broadcasted_iota(jnp.int32, (tok.shape[0], table.shape[0]), 1)
    one_hot = (tok == ids).astype(BF16)
    return jnp.dot(one_hot, table, preferred_element_type=F32)


def edge_kernel(tok_ref, table_ref, key_ref, out_ref):
    out_ref[...] = (key_ref[...].astype(F32) * embed(tok_ref[...], table_ref[...])).astype(BF16)


def se_kernel(tok_ref, table_ref, edge_ref, query_ref, key_ref, filt_ref, next_ref, stream_out, input_out, tail_out):
    emb = embed(tok_ref[...], table_ref[...])
    rows = emb.shape[0]
    gated = (key_ref[...].astype(F32) * emb).astype(BF16).astype(F32)
    edge = edge_ref[...].astype(F32)
    halo = edge.shape[0]
    padded = jnp.concatenate([edge, gated], 0)
    weights = filt_ref[...]
    conv = gated * weights[0:1, :]
    for k in range(1, weights.shape[0]):
        conv = conv + padded[halo - k : halo - k + rows] * weights[k : k + 1, :]
    stream = (emb + query_ref[...].astype(F32) * conv).astype(BF16)
    stream_out[...] = stream
    gated = (next_ref[...].astype(F32) * stream.astype(F32)).astype(BF16)
    input_out[...] = gated
    tail_out[...] = gated[rows - tail_out.shape[0] :]


def fold_groups(res, taps, groups, width):
    lane_group = lane_groups(taps, res.shape[1], width)
    total = res[0:taps]
    for g in range(1, groups):
        total = jnp.where(lane_group == g, res[g * taps : (g + 1) * taps], total)
    return total


def conv_kernel(where_ref, mr_tab, li_tab, in_ref, halo_ref, stream_ref, mrq_ref, lik_ref, liq_ref, *outs):
    step = pl.program_id(0)
    at = lax.rem(where_ref[0] + step, len(outs))
    taps = halo_ref.shape[0]
    groups = mr_tab.shape[1] // taps
    modes = li_tab.shape[1] // groups - taps
    width = LANES // groups
    near, far = in_ref[0:taps, :], in_ref[taps:, :]
    right = jnp.concatenate([near, far], 0)
    pair = jnp.concatenate([jnp.concatenate([halo_ref[...], near], 0), right], 1)
    res = jnp.dot(mr_tab[at], pair, preferred_element_type=F32)
    both = fold_groups(res, taps, groups, width)
    conv = jnp.concatenate([both[:, :LANES], both[:, LANES:]], 0)
    stream = (stream_ref[...].astype(F32) + mrq_ref[...].astype(F32) * conv).astype(BF16)
    stream_f = stream.astype(F32)
    gated = (lik_ref[...].astype(F32) * stream_f).astype(BF16)
    near = gated[0:taps, :]
    pair = jnp.concatenate([jnp.concatenate([jnp.zeros_like(near), near], 0), gated], 1)
    res = jnp.dot(li_tab[at], pair, preferred_element_type=F32)
    both = fold_groups(res, taps, groups, width)
    conv = jnp.concatenate([both[:, :LANES], both[:, LANES:]], 0)
    rows = conv.shape[0]
    wide = (stream_f + liq_ref[...].astype(F32) * conv).astype(BF16)
    ends = res[groups * taps :, LANES:].reshape(modes, groups, LANES)
    mine = lax.broadcasted_iota(jnp.int32, (modes, groups, LANES), 2) // width
    mine = mine == lax.broadcasted_iota(jnp.int32, (modes, groups, LANES), 1)
    state = jnp.sum(jnp.where(mine, ends, 0.0), axis=1)
    high = state.astype(BF16)
    low = (state - high.astype(F32)).astype(BF16)
    for s, out_ref in enumerate(outs):

        @pl.when(step == s)
        def _():
            out_ref[0:rows, :] = wide
            out_ref[rows : rows + modes, :] = high
            out_ref[rows + modes : rows + 2 * modes, :] = low


def pack_kernel(a_ref, b_ref, c_ref, out_ref):
    rows = a_ref.shape[0]
    for j in range(out_ref.shape[0]):
        for n, ref in enumerate((a_ref, b_ref, c_ref)):
            out_ref[j, n * rows : (n + 1) * rows, :] = ref[:, j * HEAD : (j + 1) * HEAD]


def unpack(where, parts, cuts):
    count = len(parts)
    bounds = list(zip((0,) + cuts[:-1], cuts))
    parts = [part.reshape(cuts[-1], LANES) for part in parts]

    def body(where_ref, *refs):
        for s in range(count):
            z = lax.rem(where_ref[0] + count - s, count)
            for (low, high), out_ref in zip(bounds, refs[count:]):
                out_ref[z] = refs[s][low:high, :]

    sizes = [(count, high - low, LANES) for low, high in bounds]
    return pl.pallas_call(
        body,
        grid=(1,),
        in_specs=[pl.BlockSpec(memory_space=pltpu.SMEM)] + [whole((cuts[-1], LANES))] * count,
        out_specs=[whole(size) for size in sizes],
        out_shape=[jax.ShapeDtypeStruct(size, BF16) for size in sizes],
    )(where, *parts)


def value_kernel(where_ref, pack_ref, all_ref, liq_ref, s1_ref, s2_ref, s3_ref, rate_ref, res_ref,
                 total_len, out_ref, emit):
    blocks, rows, _ = out_ref.shape
    modes = rate_ref.shape[0]
    x = where_ref[1]
    rate = rate_ref[...]
    step = (lax.broadcasted_iota(jnp.int32, (rows, LANES), 0) + 1).astype(F32)

    @pl.loop(0, modes)
    def _(m):
        slow, strength = rate_ref[pl.ds(m, 1), :], res_ref[pl.ds(m, 1), :]
        strength = strength * jnp.sqrt(1.0 - jnp.exp(-2.0 * slow) + 1.0 / total_len)
        emit[m] = strength * jnp.exp(-slow * step)

    decays = [jnp.exp(-rate * (rows * k)) for k in range(STRIPE + 1)]
    scans = []
    for part in (all_ref, s1_ref, s2_ref, s3_ref):
        running = jnp.zeros((modes, LANES), F32)
        seen = [running]
        for b in range(blocks):
            here = part[b, 0:modes, :].astype(F32) + part[b, modes : 2 * modes, :].astype(F32)
            running = running * decays[STRIPE] + here
            seen.append(running)
        scans.append(seen)
    carries = []
    for b in range(blocks):
        total = decays[STRIPE - 1] * scans[0][b]
        for k in range(1, STRIPE):
            total = total + decays[k - 1] * jnp.where(x >= k, scans[k][b + 1], scans[k][b])
        carries.append(total)
    piece = 32

    @pl.loop(0, rows // piece)
    def _(r):
        place = pl.ds(pl.multiple_of(r * piece, piece), piece)
        convs = [jnp.zeros((piece, LANES), F32)] * blocks
        for m in range(modes):
            table = emit[m, place, :]
            convs = [conv + table * carries[b][m : m + 1, :] for b, conv in enumerate(convs)]
        for b, conv in enumerate(convs):
            out_ref[b, place, :] = (
                pack_ref[b, place, :].astype(F32) + liq_ref[b, place, :].astype(F32) * conv
            ).astype(BF16)


def causal(scores, x, k, rows):
    head = scores[:rows]
    if k == 0:
        row = lax.broadcasted_iota(jnp.int32, head.shape, 0)
        col = lax.broadcasted_iota(jnp.int32, head.shape, 1)
        head = jnp.where(col <= row, head, -1e30)
    else:
        head = jnp.where(x >= k, head, -1e30)
    if scores.shape[0] == rows:
        return head
    return jnp.concatenate([head, scores[rows:]], 0)


def products(where_ref, q_ref, refs, use):
    depth, rows, _ = q_ref.shape
    x = where_ref[1]
    for g in range(depth):
        query = q_ref[g:].reshape((depth - g) * rows, HEAD)
        for n, (k, first, ref) in enumerate(refs):
            if first <= g < first + ref.shape[0]:
                scores = lax.dot_general(
                    query, ref[g - first], (((1,), (1,)), ((), ())), preferred_element_type=F32
                )
                use(g, n, causal(scores, x, k, rows))


def peak_kernel(where_ref, q_ref, k0, k1, k2, k3, k4, peak_out, top_ref):
    depth, rows, _ = q_ref.shape
    top_ref[...] = jnp.full(top_ref.shape, -1e30, F32)

    def use(g, n, scores):
        top = jnp.maximum(scores[:, :LANES], scores[:, LANES:])
        top_ref[g * rows :] = jnp.maximum(top_ref[g * rows :], top)

    half = depth // 2
    refs = ((0, 0, k0), (1, 0, k1), (2, 0, k2), (2, half, k3), (3, 0, k4))
    products(where_ref, q_ref, refs, use)
    for i in range(depth):
        part = jnp.max(top_ref[i * rows : (i + 1) * rows], axis=1, keepdims=True)
        peak_out[i * rows : (i + 1) * rows] = jnp.broadcast_to(part * FACTOR, (rows, LANES))


def gather_up(where_ref, q_ref, peak_ref, refs, values, acc_ref, sum_ref):
    rows = q_ref.shape[1]

    def use(g, n, scores):
        shift = peak_ref[g * rows :]
        low = jnp.exp2(scores[:, :LANES] * FACTOR - shift)
        high = jnp.exp2(scores[:, LANES:] * FACTOR - shift)
        sum_ref[g * rows :] = sum_ref[g * rows :] + (low + high)
        weights = jnp.concatenate([low.astype(BF16), high.astype(BF16)], 1)
        value = values[n][g - refs[n][1]]
        mixed = jnp.dot(weights, value, preferred_element_type=F32)
        acc_ref[g * rows :] = acc_ref[g * rows :] + mixed

    products(where_ref, q_ref, refs, use)


def near_kernel(where_ref, q_ref, peak_ref, k0, k1, k4, v0, v1, v4, acc_ref, sum_ref):
    acc_ref[...] = jnp.zeros(acc_ref.shape, F32)
    sum_ref[...] = jnp.zeros(sum_ref.shape, F32)
    refs = ((0, 0, k0), (1, 0, k1), (3, 0, k4))
    gather_up(where_ref, q_ref, peak_ref, refs, (v0, v1, v4), acc_ref, sum_ref)


def far_kernel(where_ref, q_ref, peak_ref, k2, k3, v2, v3, v0, acc_in, sum_in, out_ref, acc_ref, sum_ref):
    depth, rows, _ = q_ref.shape
    acc_ref[...] = acc_in[...]
    sum_ref[...] = sum_in[...]
    refs = ((2, 0, k2), (2, depth // 2, k3))
    gather_up(where_ref, q_ref, peak_ref, refs, (v2, v3), acc_ref, sum_ref)
    for i in range(depth):
        place = slice(i * rows, (i + 1) * rows)
        total = jnp.sum(sum_ref[place], axis=1, keepdims=True)
        attended = (acc_ref[place] / total).astype(BF16)
        out_ref[i] = (v0[i].astype(F32) + attended.astype(F32)).astype(BF16)


def whole(shape):
    return pl.BlockSpec(shape, lambda *_: (0,) * len(shape))


def local(
    token_ids,
    embed_table,
    se_query,
    se_key,
    se_filter,
    mr_query,
    mr_key,
    mr_filter,
    li_query,
    li_key,
    li_rate,
    li_residue,
    attn_query,
    attn_key,
):
    rows = token_ids.shape[0]
    vocab, channels = embed_table.shape
    group_count = se_filter.shape[0]
    width = channels // group_count
    seq = lax.axis_size("seq")
    total_len = rows * seq
    heads = channels // HEAD
    depth = seq // STRIPE
    taps = mr_filter.shape[1]
    modes = li_rate.shape[1]
    here = lax.axis_index("seq")
    where = jnp.stack([here // STRIPE, here % STRIPE]).astype(jnp.int32)
    smem = pl.BlockSpec(memory_space=pltpu.SMEM)
    columns = [[z * STRIPE + x for z in range(depth)] for x in range(STRIPE)]
    forward = [(d, d + 1) for d in range(seq - 1)]

    def turn(shift):
        return [(d, d // STRIPE * STRIPE + (d + shift) % STRIPE) for d in range(seq)]

    def exchange(packed):
        return lax.all_to_all(
            packed, "seq", split_axis=0, concat_axis=0, tiled=True, axis_index_groups=columns
        )

    def shifted(parts):
        return [parts[0]] + [
            lax.ppermute(
                part, "seq", [(d, (d // STRIPE + s) % depth * STRIPE + d % STRIPE) for d in range(seq)]
            )
            for s, part in enumerate(parts)
            if s
        ]

    def spread(part):
        behind = lax.ppermute(part, "seq", turn(1))
        ahead = lax.ppermute(part, "seq", turn(STRIPE - 1))
        half = depth // 2
        across = [
            lax.ppermute(behind[:half], "seq", turn(1)),
            lax.ppermute(ahead[half:], "seq", turn(STRIPE - 1)),
        ]
        return part, behind, *across, ahead

    inside = pl.BlockSpec(memory_space=pltpu.VMEM)
    small = pltpu.CompilerParams(vmem_limit_bytes=16 * MIB)
    early = pl.pallas_call(
        pack_kernel,
        grid=(2,),
        in_specs=[pl.BlockSpec((rows, channels // 2), lambda j: (0, j))] * 3,
        out_specs=pl.BlockSpec((heads // 2, 3 * rows, HEAD), lambda j: (j, 0, 0)),
        out_shape=jax.ShapeDtypeStruct((heads, 3 * rows, HEAD), BF16),
        name="pack",
    )(attn_query, attn_key, li_query)

    tok = token_ids[:, None]
    halo = 8
    last = rows // halo - 1
    edge = pl.pallas_call(
        edge_kernel,
        grid=(1,),
        in_specs=[
            pl.BlockSpec((halo, 1), lambda i: (last, 0)),
            whole((vocab, channels)),
            pl.BlockSpec((halo, channels), lambda i: (last, 0)),
        ],
        out_specs=whole((halo, channels)),
        out_shape=jax.ShapeDtypeStruct((halo, channels), BF16),
        name="edge",
    )(tok, embed_table, se_key)
    edge = lax.ppermute(edge, "seq", forward)

    mr_tab, li_tab = make_tables(mr_filter, li_rate, li_residue, total_len)

    se_taps = se_filter.shape[1]
    se_weights = jnp.broadcast_to(
        se_filter.astype(F32).T[:, :, None], (se_taps, group_count, width)
    ).reshape(se_taps, channels)
    wide = 256
    column = pl.BlockSpec((rows, wide), lambda j: (0, j))
    stream, mr_input, mr_tail = pl.pallas_call(
        se_kernel,
        grid=(channels // wide,),
        in_specs=[
            whole((rows, 1)),
            pl.BlockSpec((vocab, wide), lambda j: (0, j)),
            pl.BlockSpec((halo, wide), lambda j: (0, j)),
            column,
            column,
            pl.BlockSpec((se_taps, wide), lambda j: (0, j)),
            column,
        ],
        out_specs=[column, column, pl.BlockSpec((taps, wide), lambda j: (0, j))],
        out_shape=[jax.ShapeDtypeStruct((rows, channels), BF16)] * 2
        + [jax.ShapeDtypeStruct((taps, channels), BF16)],
        name="short",
    )(tok, embed_table, edge, se_query, se_key, se_weights, mr_key)
    mr_edge = lax.ppermute(mr_tail, "seq", forward)
    early = exchange(early)

    column = pl.BlockSpec((rows, LANES), lambda j, w: (0, lax.rem(w[0] + j, heads)))
    ends = pl.BlockSpec((taps, LANES), lambda j, w: (0, lax.rem(w[0] + j, heads)))
    size = (rows + 2 * modes, LANES)
    packed = pl.pallas_call(
        conv_kernel,
        grid_spec=pltpu.PrefetchScalarGridSpec(
            num_scalar_prefetch=1,
            grid=(heads,),
            in_specs=[inside, inside, column, ends, column, column, column, column],
            out_specs=[pl.BlockSpec(size, lambda j, w: (0, 0))] * heads,
        ),
        out_shape=[jax.ShapeDtypeStruct(size, BF16)] * heads,
        compiler_params=pltpu.CompilerParams(vmem_limit_bytes=24 * MIB),
        name="medium_long",
    )(where, mr_tab, li_tab, mr_input, mr_edge, stream, mr_query, li_key, li_query)
    packed = shifted(packed)

    query, key, early_gate = (early[:, n * rows : (n + 1) * rows] for n in range(3))
    keys = spread(key)
    packed, states = unpack(where, packed, (rows, rows + 2 * modes))
    others = [lax.ppermute(states, "seq", turn(k)) for k in range(1, STRIPE)]

    def mine(value):
        count = HEAD // width
        value = lax.dynamic_slice_in_dim(value, where[0] * count, count, axis=0)
        value = jnp.broadcast_to(value.T[:, :, None], (modes, count, width))
        return value.reshape(modes, HEAD)

    def value_body(*refs):
        value_kernel(*refs[:9], total_len, *refs[9:])

    values = pl.pallas_call(
        value_body,
        in_specs=[smem] + [inside] * 8,
        out_specs=inside,
        out_shape=jax.ShapeDtypeStruct((depth, rows, LANES), BF16),
        scratch_shapes=[pltpu.VMEM((modes, rows, LANES), F32)],
        compiler_params=small,
        name="values",
    )(where, packed, states, early_gate, *others, mine(li_rate), mine(li_residue))
    values = spread(values)

    reach = depth * rows
    peaks = pl.pallas_call(
        peak_kernel,
        in_specs=[smem] + [inside] * 6,
        out_specs=inside,
        out_shape=jax.ShapeDtypeStruct((reach, LANES), F32),
        scratch_shapes=[pltpu.VMEM((reach, LANES), F32)],
        compiler_params=pltpu.CompilerParams(vmem_limit_bytes=30 * MIB),
        name="peaks",
    )(where, query, *keys)
    k0, k1, k2, k3, k4 = keys
    v0, v1, v2, v3, v4 = values
    sums = jax.ShapeDtypeStruct((reach, LANES), F32)
    near = pl.pallas_call(
        near_kernel,
        in_specs=[smem] + [inside] * 8,
        out_specs=[inside, inside],
        out_shape=[sums, sums],
        compiler_params=pltpu.CompilerParams(vmem_limit_bytes=40 * MIB),
        name="near",
    )(where, query, peaks, k0, k1, k4, v0, v1, v4)
    result = pl.pallas_call(
        far_kernel,
        in_specs=[smem] + [inside] * 9,
        out_specs=inside,
        out_shape=jax.ShapeDtypeStruct((depth, rows, HEAD), BF16),
        scratch_shapes=[pltpu.VMEM((reach, HEAD), F32), pltpu.VMEM((reach, LANES), F32)],
        compiler_params=pltpu.CompilerParams(vmem_limit_bytes=40 * MIB),
        name="far",
    )(where, query, peaks, k2, k3, v2, v3, v0, *near)
    result = exchange(result)
    return result.transpose(1, 0, 2).reshape(rows, channels)


def solution(mesh):
    wide = P("seq", "chan")
    narrow = P("chan", None)
    in_specs = (
        P("seq"), P(None, "chan"), wide, wide, narrow, wide, wide, narrow, wide, wide, narrow,
        narrow, wide, wide,
    )

    return jax.shard_map(local, mesh=mesh, in_specs=in_specs, out_specs=wide, check_vma=False)
```
